128 devices in a mesh: group: 8 (over y, core), member: 16 (over z, x).
Axes of the slice: x: 4, y: 4, z: 4, core: 2. Of those that a mesh axis runs over, the one named last changes fastest.
Arguments:
- queries: bfloat16 [512, 32, 128], P('group'), may hold values from -0.5 to 0.5
- centroids: bfloat16 [131072, 128], P('member'), may hold values from -0.5 to 0.5
- doc_resid: bfloat16 [32768, 128, 128], P(('group', 'member')), may hold values from -6 to 6
- doc_codes: int32 [32768, 128], P(('group', 'member')), may hold values from 0 to 131071
- doc_scale: bfloat16 [32768], P(('group', 'member')), may hold values from 0.019897461 to 0.19921875
- doc_len: int32 [32768], P(('group', 'member')), may hold values from 1 to 128
- send_list: int32 [128, 128, 2], P(('group', 'member')), may hold values from 0 to 255
- cand: int32 [512, 2048], P('group', 'member'), may hold values from 0 to 255
Outputs:
- scores: float32 [512, 2048], P('group', 'member')
The draws below stay inside these ranges and needn't reach their ends.
Inputs may be any that keep to these rules, and one draw needn't show every extreme that they name: `cand`: slot s names the document source s div 2 sent to this candidate's device in its slot s mod 2.
All inputs are finite; a program needn't handle non-finite values.
Results may differ from the reference program's by a relative error of at most 0.0003.
Values may be sent and summed in bfloat16 or wider, within the bound.
No kernel may reach another device: no remote copies, remote signals or barrier semaphores. Data moves between devices by JAX's collectives and lax.ppermute only.
A program may use at most 256 MiB of HBM per device.

```python
import math
import jax
import jax.numpy as jnp
import numpy as np
from jax import lax

DIM = 128
QT = 32
BLK = 128
CENT = 131072
QG = 64
DOCS_DEV = 256
CAP = 2
KM = 128
QUERIES = 512
K = 2048
DOCS = 32768
N_MEMBER = 16
DEVICES = 128


def plant(array, rng, low, top_value):
    longest = array.shape.index(max(array.shape))
    spots = []
    for shift in (0, 1):
        where = [jax.random.randint(jax.random.fold_in(rng, axis), (), 0, length) for axis, length in enumerate(array.shape)]
        where[longest] = (where[longest] + shift) % array.shape[longest]
        spots.append(tuple(where))
    return array.at[spots[0]].set(low).at[spots[1]].set(top_value)


def block_scale(rng, shape, pieces, smallest, top_value):
    level, own = 1.0, jax.random.fold_in(rng, 6)
    for dim, shards_of in pieces:
        heights = jnp.exp(jax.random.uniform(jax.random.fold_in(own, dim), (shards_of,), jnp.float32, smallest / len(pieces), top_value / len(pieces)))
        level = level * jnp.repeat(heights, shape[dim] // shards_of).reshape([-1 if axis == dim else 1 for axis in range(len(shape))])
    return level


def wide_ids(key, extent, count, slope):
    portions = [min(1 << octave, count + 1 - (1 << octave)) * (1 << 20) // math.isqrt((1 << octave) ** slope) + 1 for octave in range((count + 1).bit_length()) if 1 << octave <= count]
    scale = 1 + sum(portions) // (1 << 30)
    table = np.cumsum(np.array([max(1, weight // scale) for weight in portions]))
    pick = jax.random.randint(jax.random.fold_in(key, 1), extent, 0, int(table[len(portions) - 1]))
    start = jnp.left_shift(1, jnp.searchsorted(jnp.asarray(table, jnp.int32), pick, side="right").astype(jnp.int32))
    grade = start - 1 + jax.random.randint(jax.random.fold_in(key, 4), extent, 0, 1 << 30) % jnp.minimum(start, count + 1 - start)
    return jax.random.permutation(jax.random.fold_in(key, 2), count)[grade].astype(jnp.int32)


def scatter_about(stream_key, shape, scale, limit, pieces=(), held_as=jnp.bfloat16):
    result = scale * jax.random.normal(stream_key, shape, jnp.float32)
    if pieces:
        result = result * block_scale(stream_key, shape, pieces, -0.22, 0.18)
    return jnp.clip(result, -limit, limit).astype(held_as)


def setup_inputs(seed: int = 0) -> dict:
    streams_of = jax.random.split(jax.random.key(seed), 9)
    return {
        "queries": scatter_about(streams_of[0], (QUERIES, QT, DIM), DIM ** -0.5, 0.5, ((0, 8),)),
        "centroids": scatter_about(streams_of[1], (CENT, DIM), DIM ** -0.5, 0.5, ((0, 16),)),
        "doc_resid": scatter_about(streams_of[2], (DOCS, BLK, DIM), 1.0, 6.0, ((0, 128),)),
        "doc_codes": plant(wide_ids(streams_of[3], (DOCS, BLK), CENT, 2), jax.random.fold_in(streams_of[3], 3), 0, CENT - 1).astype(jnp.int32),
        "doc_scale": jnp.clip(jnp.exp(math.log(0.19921875) - 2.3038113 * jax.random.uniform(streams_of[4], (DOCS,), jnp.float32) ** block_scale(streams_of[4], (DOCS,), ((0, 128),), -0.2, 0.2)), 0.019897461, 0.19921875).astype(jnp.bfloat16),
        "doc_len": plant(jax.random.randint(streams_of[5], (DOCS,), 1, BLK + 1), jax.random.fold_in(streams_of[5], 1), 1, BLK).astype(jnp.int32),
        "send_list": plant(jax.random.randint(streams_of[6], (DEVICES, DEVICES, CAP), 0, DOCS_DEV), jax.random.fold_in(streams_of[6], 1), 0, DOCS_DEV - 1).astype(jnp.int32),
        "cand": plant(jax.random.randint(streams_of[7], (QUERIES, K), 0, DEVICES * CAP), jax.random.fold_in(streams_of[7], 1), 0, (DEVICES * CAP) - 1).astype(jnp.int32),
    }


def reference(queries, centroids, doc_resid, doc_codes, doc_scale, doc_len, send_list, cand):
    query_group = (jnp.arange(QUERIES, dtype=jnp.int32) // QG)[:, None]
    member_index = (jnp.arange(K, dtype=jnp.int32) // KM)[None, :]
    destination = (query_group * N_MEMBER + member_index).astype(jnp.int32)
    source = (cand // CAP).astype(jnp.int32)
    column = (cand % CAP).astype(jnp.int32)
    doc_index = (source * DOCS_DEV + send_list[source, destination, column]).astype(jnp.int32)

    def one_query(items):
        query, docs = items
        codes = doc_codes[docs]
        embedding = (centroids[codes].astype(jnp.float32)
                     + doc_scale[docs].astype(jnp.float32)[:, None, None] * doc_resid[docs].astype(jnp.float32)).astype(jnp.bfloat16)
        sims = jnp.einsum("td,kjd->ktj", query.astype(jnp.float32), embedding.astype(jnp.float32))
        valid = jnp.arange(BLK, dtype=jnp.int32)[None, :] < doc_len[docs][:, None]
        sims = jnp.where(valid[:, None, :], sims, jnp.float32(-1.0e9))
        return jnp.mean(jnp.max(sims, axis=2), axis=1)

    return lax.map(one_query, (queries, doc_index))
```

```python
import jax
import jax.numpy as jnp
from jax import lax
from jax.experimental import pallas as pl
from jax.experimental.pallas import tpu as pltpu
from jax.sharding import PartitionSpec as P

f32 = jnp.float32
bf16 = jnp.bfloat16
GROUPS = 8
HALF = 16
TOKENS = 128
QROWS = 2048
TILE = 256
TILES = QROWS // TILE


def score_kernel(place, docs, table, resid, query, odd, scale, length, out, pairs_a, pairs_b, wide, embedded):
    group = pl.program_id(0)

    def gather(pairs, first, part, parts):
        count = HALF * TOKENS // parts
        for spot in range(count * part, count * (part + 1)):
            doc, token = divmod(spot, TOKENS)
            pairs[2 * spot : 2 * spot + 2, :] = table[place[(first + doc) * TOKENS + token]]

    def embed(pairs, half):
        base = pl.multiple_of((group * 2 + half) * HALF, HALF)
        odd_t = odd[pl.ds(base, HALF), :].T
        scale_t = scale[pl.ds(base, HALF), :].T
        length_t = length[pl.ds(base, HALF), :].T
        token = lax.broadcasted_iota(jnp.int32, (TOKENS, TOKENS), 0)
        for doc in range(HALF):
            wide[...] = pairs[2 * TOKENS * doc : 2 * TOKENS * (doc + 1), :].astype(f32)
            even_rows = wide[pl.ds(0, TOKENS, stride=2), :]
            odd_rows = wide[pl.ds(1, TOKENS, stride=2), :]
            center = jnp.where(odd_t[:, doc : doc + 1] > 0, odd_rows, even_rows)
            value = center + scale_t[:, doc : doc + 1] * resid[docs[base + doc]].astype(f32)
            value = jnp.where(token < length_t[:, doc : doc + 1], value, value[0:1, :])
            embedded[TOKENS * doc : TOKENS * (doc + 1), :] = value.astype(bf16)

    def compute(half, feed):
        total = None
        for tile in range(TILES):
            feed(tile)
            sims = lax.dot_general(
                embedded[...],
                query[0, TILE * tile : TILE * (tile + 1), :],
                (((1,), (1,)), ((), ())),
                preferred_element_type=f32,
            )
            best = jnp.max(sims.reshape(HALF, TOKENS, TILE), axis=1)
            best = best[:, :128] + best[:, 128:]
            total = best if total is None else total + best
        total = (total + pltpu.roll(total, 64, 1)) * (1.0 / 32)
        lane = lax.broadcasted_iota(jnp.int32, (8, 128), 1)
        out[8 * half : 8 * half + 8, :] = jnp.where(lane < 64, total[:8], total[8:])

    @pl.when(group == 0)
    def _():
        gather(pairs_a, 0, 0, 1)

    embed(pairs_a, 0)
    compute(0, lambda tile: gather(pairs_b, (group * 2 + 1) * HALF, tile, TILES))
    embed(pairs_b, 1)
    following = jnp.minimum(group + 1, GROUPS - 1) * 2 * HALF
    compute(1, lambda tile: gather(pairs_a, following, tile, TILES))


def score(place, docs, table, resid, query, odd, scale, length):
    whole = pl.BlockSpec(memory_space=pltpu.VMEM)
    return pl.pallas_call(
        score_kernel,
        grid_spec=pltpu.PrefetchScalarGridSpec(
            num_scalar_prefetch=2,
            grid=(GROUPS,),
            in_specs=[
                whole,
                whole,
                pl.BlockSpec((1, QROWS, 128), lambda group, *_: (group, 0, 0)),
                whole,
                whole,
                whole,
            ],
            out_specs=pl.BlockSpec((16, 128), lambda group, *_: (group, 0)),
            scratch_shapes=[
                pltpu.VMEM((HALF * TOKENS * 2, 128), bf16),
                pltpu.VMEM((HALF * TOKENS * 2, 128), bf16),
                pltpu.VMEM((TOKENS * 2, 128), f32),
                pltpu.VMEM((HALF * TOKENS, 128), bf16),
            ],
        ),
        out_shape=jax.ShapeDtypeStruct((128, 128), f32),
        compiler_params=pltpu.CompilerParams(vmem_limit_bytes=60 << 20),
        name="score",
    )(place, docs, table, resid, query, odd, scale, length)


def pick_kernel(held, cand, out):
    turned = held[...].T
    source = cand[...] // 2
    first = jnp.take_along_axis(turned[:64], source, axis=1, mode="promise_in_bounds")
    second = jnp.take_along_axis(turned[64:], source, axis=1, mode="promise_in_bounds")
    out[...] = jnp.where(cand[...] % 2 == 0, first, second)


def pick(held, cand):
    return pl.pallas_call(
        pick_kernel, out_shape=jax.ShapeDtypeStruct((64, 128), f32), name="pick"
    )(held, cand)


def body(queries, centroids, doc_resid, doc_codes, doc_scale, doc_len, send_list, cand):
    axes = ("group", "member")
    group = lax.axis_index("group")
    part = lax.dynamic_slice_in_dim(centroids, group * 1024, 1024, 0)
    table = lax.all_gather(part.reshape(512, 2, 128), axes, axis=0, tiled=True)
    turned = queries.transpose(1, 0, 2).reshape(QROWS, 128)
    query = lax.all_gather(turned, "group", axis=0)
    docs = send_list[0].reshape(8, 2, 8, 2).transpose(0, 1, 3, 2).reshape(-1)
    codes = jnp.take(doc_codes, docs, axis=0, mode="clip")
    row = (((codes >> 10) & 7) * 16 + (codes >> 13)) * 1024 + (codes & 1023)
    scale = jnp.take(doc_scale, docs, axis=0, mode="clip").astype(f32)
    length = jnp.take(doc_len, docs, axis=0, mode="clip")
    spread = lambda x: jnp.broadcast_to(x[:, None], (256, 128))
    scores = score(
        (row >> 1).reshape(-1), docs, table, doc_resid, query, row & 1, spread(scale), spread(length)
    )
    held = lax.all_to_all(scores, axes, split_axis=0, concat_axis=0, tiled=True)
    return pick(held, cand)


def solution(mesh):
    placed = (
        P("group", None, None),
        P("member", None),
        P(("group", "member"), None, None),
        P(("group", "member"), None),
        P(("group", "member")),
        P(("group", "member")),
        P(("group", "member"), None, None),
        P("group", "member"),
    )
    return jax.shard_map(
        body, mesh=mesh, in_specs=placed, out_specs=P("group", "member"), check_vma=False
    )
```

```python
import jax
import jax.numpy as jnp
from jax import lax
from jax.experimental import pallas as pl
from jax.experimental.pallas import tpu as pltpu
from jax.sharding import PartitionSpec as P

f32 = jnp.float32
bf16 = jnp.bfloat16
GROUPS = 8
HALF = 16
TOKENS = 128
QROWS = 2048
TILE = 256
TILES = QROWS // TILE


def score_kernel(own, place, docs, table, resid, query, odd, scale, length, out, pairs_a, pairs_b, wide, embedded):
    group = pl.program_id(0)

    def gather(pairs, first, part, parts):
        count = HALF * TOKENS // parts
        for spot in range(count * part, count * (part + 1)):
            doc, token = divmod(spot, TOKENS)
            pairs[2 * spot : 2 * spot + 2, :] = table[place[(first + doc) * TOKENS + token]]

    def embed(pairs, half):
        base = pl.multiple_of((group * 2 + half) * HALF, HALF)
        odd_t = odd[pl.ds(base, HALF), :].T
        scale_t = scale[pl.ds(base, HALF), :].T
        length_t = length[pl.ds(base, HALF), :].T
        token = lax.broadcasted_iota(jnp.int32, (TOKENS, TOKENS), 0)
        for doc in range(HALF):
            wide[...] = pairs[2 * TOKENS * doc : 2 * TOKENS * (doc + 1), :].astype(f32)
            even_rows = wide[pl.ds(0, TOKENS, stride=2), :]
            odd_rows = wide[pl.ds(1, TOKENS, stride=2), :]
            center = jnp.where(odd_t[:, doc : doc + 1] > 0, odd_rows, even_rows)
            value = center + scale_t[:, doc : doc + 1] * resid[docs[base + doc]].astype(f32)
            value = jnp.where(token < length_t[:, doc : doc + 1], value, value[0:1, :])
            embedded[TOKENS * doc : TOKENS * (doc + 1), :] = value.astype(bf16)

    def compute(half, feed):
        total = None
        for tile in range(TILES):
            feed(tile)
            sims = lax.dot_general(
                embedded[...],
                query[0, TILE * tile : TILE * (tile + 1), :],
                (((1,), (1,)), ((), ())),
                preferred_element_type=f32,
            )
            best = jnp.max(sims.reshape(HALF, TOKENS, TILE), axis=1)
            best = best[:, :128] + best[:, 128:]
            total = best if total is None else total + best
        total = (total + pltpu.roll(total, 64, 1)) * (1.0 / 32)
        lane = lax.broadcasted_iota(jnp.int32, (8, 128), 1)
        out[8 * half : 8 * half + 8, :] = jnp.where(lane < 64, total[:8], total[8:])

    @pl.when(group == 0)
    def _():
        gather(pairs_a, 0, 0, 1)

    embed(pairs_a, 0)
    compute(0, lambda tile: gather(pairs_b, (group * 2 + 1) * HALF, tile, TILES))
    embed(pairs_b, 1)
    following = jnp.minimum(group + 1, GROUPS - 1) * 2 * HALF
    compute(1, lambda tile: gather(pairs_a, following, tile, TILES))


def score(own, place, docs, table, resid, query, odd, scale, length):
    whole = pl.BlockSpec(memory_space=pltpu.VMEM)
    return pl.pallas_call(
        score_kernel,
        grid_spec=pltpu.PrefetchScalarGridSpec(
            num_scalar_prefetch=3,
            grid=(GROUPS,),
            in_specs=[
                whole,
                whole,
                pl.BlockSpec((1, QROWS, 128), lambda group, own, *_: (group ^ own[0], 0, 0)),
                whole,
                whole,
                whole,
            ],
            out_specs=pl.BlockSpec((16, 128), lambda group, *_: (group, 0)),
            scratch_shapes=[
                pltpu.VMEM((HALF * TOKENS * 2, 128), bf16),
                pltpu.VMEM((HALF * TOKENS * 2, 128), bf16),
                pltpu.VMEM((TOKENS * 2, 128), f32),
                pltpu.VMEM((HALF * TOKENS, 128), bf16),
            ],
        ),
        out_shape=jax.ShapeDtypeStruct((128, 128), f32),
        compiler_params=pltpu.CompilerParams(vmem_limit_bytes=60 << 20),
        name="score",
    )(own, place, docs, table, resid, query, odd, scale, length)


def pick_kernel(held, cand, out):
    turned = held[...].T
    source = cand[...] // 2
    first = jnp.take_along_axis(turned[:64], source, axis=1, mode="promise_in_bounds")
    second = jnp.take_along_axis(turned[64:], source, axis=1, mode="promise_in_bounds")
    out[...] = jnp.where(cand[...] % 2 == 0, first, second)


def pick(held, cand):
    return pl.pallas_call(
        pick_kernel, out_shape=jax.ShapeDtypeStruct((64, 128), f32), name="pick"
    )(held, cand)


def body(queries, centroids, doc_resid, doc_codes, doc_scale, doc_len, send_list, cand):
    axes = ("group", "member")
    group = lax.axis_index("group")
    part = lax.dynamic_slice_in_dim(centroids, group * 1024, 1024, 0)
    table = lax.all_gather(part.reshape(512, 2, 128), axes, axis=0, tiled=True)
    turned = queries.transpose(1, 0, 2).reshape(QROWS, 128)
    query = turned[None]
    for step in (1, 2, 4):
        swapped = lax.ppermute(query, "group", [(g, g ^ step) for g in range(GROUPS)])
        query = jnp.concatenate([query, swapped], axis=0)
    docs = send_list[0].reshape(8, 2, 8, 2).transpose(0, 1, 3, 2).reshape(-1)
    codes = jnp.take(doc_codes, docs, axis=0, mode="clip")
    row = (((codes >> 10) & 7) * 16 + (codes >> 13)) * 1024 + (codes & 1023)
    scale = jnp.take(doc_scale, docs, axis=0, mode="clip").astype(f32)
    length = jnp.take(doc_len, docs, axis=0, mode="clip")
    spread = lambda x: jnp.broadcast_to(x[:, None], (256, 128))
    scores = score(
        group[None].astype(jnp.int32),
        (row >> 1).reshape(-1), docs, table, doc_resid, query, row & 1, spread(scale), spread(length)
    )
    held = lax.all_to_all(scores, axes, split_axis=0, concat_axis=0, tiled=True)
    return pick(held, cand)


def solution(mesh):
    placed = (
        P("group", None, None),
        P("member", None),
        P(("group", "member"), None, None),
        P(("group", "member"), None),
        P(("group", "member")),
        P(("group", "member")),
        P(("group", "member"), None, None),
        P("group", "member"),
    )
    return jax.shard_map(
        body, mesh=mesh, in_specs=placed, out_specs=P("group", "member"), check_vma=False
    )
```

```python
import jax
import jax.numpy as jnp
from jax import lax
from jax.experimental import pallas as pl
from jax.experimental.pallas import tpu as pltpu
from jax.sharding import PartitionSpec as P

f32 = jnp.float32
bf16 = jnp.bfloat16
GROUPS = 8
HALF = 16
TOKENS = 128
QROWS = 2048
TILE = 256
SENT = 1152
TILES = QROWS // TILE


def score_kernel(place, docs, table, resid, query, odd, scale, length, out, pairs_a, pairs_b, wide, embedded):
    group = pl.program_id(0)

    def gather(pairs, first, part, parts):
        count = HALF * TOKENS // parts
        for spot in range(count * part, count * (part + 1)):
            doc, token = divmod(spot, TOKENS)
            pairs[2 * spot : 2 * spot + 2, :] = table[place[(first + doc) * TOKENS + token]]

    def embed(pairs, half):
        base = pl.multiple_of((group * 2 + half) * HALF, HALF)
        odd_t = odd[pl.ds(base, HALF), :].T
        scale_t = scale[pl.ds(base, HALF), :].T
        length_t = length[pl.ds(base, HALF), :].T
        token = lax.broadcasted_iota(jnp.int32, (TOKENS, TOKENS), 0)
        for doc in range(HALF):
            wide[...] = pairs[2 * TOKENS * doc : 2 * TOKENS * (doc + 1), :].astype(f32)
            even_rows = wide[pl.ds(0, TOKENS, stride=2), :]
            odd_rows = wide[pl.ds(1, TOKENS, stride=2), :]
            center = jnp.where(odd_t[:, doc : doc + 1] > 0, odd_rows, even_rows)
            value = center + scale_t[:, doc : doc + 1] * resid[docs[base + doc]].astype(f32)
            value = jnp.where(token < length_t[:, doc : doc + 1], value, value[0:1, :])
            embedded[TOKENS * doc : TOKENS * (doc + 1), :] = value.astype(bf16)

    def compute(half, feed):
        total = None
        for tile in range(TILES):
            feed(tile)
            sims = lax.dot_general(
                embedded[...],
                query[0, 2 * tile : 2 * tile + 2].reshape(TILE, 128),
                (((1,), (1,)), ((), ())),
                preferred_element_type=f32,
            )
            best = jnp.max(sims.reshape(HALF, TOKENS, TILE), axis=1)
            best = best[:, :128] + best[:, 128:]
            total = best if total is None else total + best
        total = (total + pltpu.roll(total, 64, 1)) * (1.0 / 32)
        lane = lax.broadcasted_iota(jnp.int32, (8, 128), 1)
        out[8 * half : 8 * half + 8, :] = jnp.where(lane < 64, total[:8], total[8:])

    @pl.when(group == 0)
    def _():
        gather(pairs_a, 0, 0, 1)

    embed(pairs_a, 0)
    compute(0, lambda tile: gather(pairs_b, (group * 2 + 1) * HALF, tile, TILES))
    embed(pairs_b, 1)
    following = jnp.minimum(group + 1, GROUPS - 1) * 2 * HALF
    compute(1, lambda tile: gather(pairs_a, following, tile, TILES))


def score(place, docs, table, resid, query, odd, scale, length):
    whole = pl.BlockSpec(memory_space=pltpu.VMEM)
    return pl.pallas_call(
        score_kernel,
        grid_spec=pltpu.PrefetchScalarGridSpec(
            num_scalar_prefetch=2,
            grid=(GROUPS,),
            in_specs=[
                whole,
                whole,
                pl.BlockSpec((1, 16, 128, 128), lambda group, *_: (group, 0, 8, 0)),
                whole,
                whole,
                whole,
            ],
            out_specs=pl.BlockSpec((16, 128), lambda group, *_: (group, 0)),
            scratch_shapes=[
                pltpu.VMEM((HALF * TOKENS * 2, 128), bf16),
                pltpu.VMEM((HALF * TOKENS * 2, 128), bf16),
                pltpu.VMEM((TOKENS * 2, 128), f32),
                pltpu.VMEM((HALF * TOKENS, 128), bf16),
            ],
        ),
        out_shape=jax.ShapeDtypeStruct((128, 128), f32),
        compiler_params=pltpu.CompilerParams(vmem_limit_bytes=60 << 20),
        name="score",
    )(place, docs, table, resid, query, odd, scale, length)


def pick_kernel(held, cand, out):
    turned = held[...].T
    source = cand[...] // 2
    first = jnp.take_along_axis(turned[:64], source, axis=1, mode="promise_in_bounds")
    second = jnp.take_along_axis(turned[64:], source, axis=1, mode="promise_in_bounds")
    out[...] = jnp.where(cand[...] % 2 == 0, first, second)


def pick(held, cand):
    return pl.pallas_call(
        pick_kernel, out_shape=jax.ShapeDtypeStruct((64, 128), f32), name="pick"
    )(held, cand)


def body(queries, centroids, doc_resid, doc_codes, doc_scale, doc_len, send_list, cand):
    axes = ("group", "member")
    group = lax.axis_index("group")
    part = lax.dynamic_slice_in_dim(centroids, group * 1024, 1024, 0)
    turned = queries.transpose(1, 0, 2).reshape(QROWS, 128)
    own = lax.dynamic_slice_in_dim(turned, lax.axis_index("member") * 128, 128, 0)
    sent = jnp.concatenate([part, own], axis=0)
    held = lax.all_gather(sent, axes, axis=0, tiled=True)
    table = held.reshape(-1, 2, 128)
    query = held.reshape(GROUPS, 16, SENT, 128)
    docs = send_list[0].reshape(8, 2, 8, 2).transpose(0, 1, 3, 2).reshape(-1)
    codes = jnp.take(doc_codes, docs, axis=0, mode="clip")
    row = (((codes >> 10) & 7) * 16 + (codes >> 13)) * SENT + (codes & 1023)
    scale = jnp.take(doc_scale, docs, axis=0, mode="clip").astype(f32)
    length = jnp.take(doc_len, docs, axis=0, mode="clip")
    spread = lambda x: jnp.broadcast_to(x[:, None], (256, 128))
    scores = score(
        (row >> 1).reshape(-1), docs, table, doc_resid, query, row & 1, spread(scale), spread(length)
    )
    held = lax.all_to_all(scores, axes, split_axis=0, concat_axis=0, tiled=True)
    return pick(held, cand)


def solution(mesh):
    placed = (
        P("group", None, None),
        P("member", None),
        P(("group", "member"), None, None),
        P(("group", "member"), None),
        P(("group", "member")),
        P(("group", "member")),
        P(("group", "member"), None, None),
        P("group", "member"),
    )
    return jax.shard_map(
        body, mesh=mesh, in_specs=placed, out_specs=P("group", "member"), check_vma=False
    )
```
